32 devices in a mesh: tm: 4 (over y, x), row: 4 (over z), col: 2 (over core).
Axes of the slice: x: 2, y: 2, z: 4, core: 2. Of those that a mesh axis runs over, the one named last changes fastest.
Arguments:
- features: bfloat16 [8, 16, 20, 384], P('tm', 'row', 'col'), may hold values from -6 to 6
- reward_grad: bfloat16 [8, 16, 20, 384], P('tm', 'row', 'col'), may hold values from -6 to 6
- first_kernel: bfloat16 [3, 3, 3, 384, 384], P(None, None, None, 'tm'), may hold values from -0.0625 to 0.0625
- second_kernel: bfloat16 [3, 3, 3, 384, 384], P(None, None, None, 'tm'), may hold values from -0.0625 to 0.0625
- first_gain: float32 [384], replicated, may hold values from 0.25 to 1.75
- second_gain: float32 [384], replicated, may hold values from 0.25 to 1.75
- first_bias: float32 [384], replicated, may hold values from -3 to 3
Outputs:
- input_grad: bfloat16 [8, 16, 20, 384], P('tm', 'row', 'col')
The draws below stay inside these ranges and needn't reach their ends.
All inputs are finite; a program needn't handle non-finite values.
Results may differ from the reference program's by a relative error of at most 0.0037.
Values may be sent and summed in bfloat16 or wider, within the bound.
No kernel may reach another device: no remote copies, remote signals or barrier semaphores. Data moves between devices by JAX's collectives and lax.ppermute only.
A program may use at most 128 MiB of HBM per device.

```python
import jax
import jax.numpy as jnp
from jax import lax

C = 384
FRAMES = 8
HEIGHT = 16
WIDTH = 20


def block_levels(key, dims, pieces, smallest, largest):
    level, own = 1.0, jax.random.fold_in(key, 6)
    for position, blocks in pieces:
        heights = jnp.exp(jax.random.uniform(jax.random.fold_in(own, position), (blocks,), jnp.float32, smallest / len(pieces), largest / len(pieces)))
        level = level * jnp.repeat(heights, dims[position] // blocks).reshape([-1 if axis == position else 1 for axis in range(len(dims))])
    return level


def gaussian(rng, dims, spread, reach, split=(), held_as=jnp.bfloat16):
    values = spread * jax.random.normal(rng, dims, jnp.float32)
    if split:
        values = values * block_levels(rng, dims, split, -0.22, 0.18)
    return jnp.clip(values, -reach, reach).astype(held_as)


def setup_inputs(seed: int = 0) -> dict:
    splits = jax.random.split(jax.random.key(seed), 8)
    return {
        "features": gaussian(splits[0], (FRAMES, HEIGHT, WIDTH, C), 1.0, 6.0, ((0, 4), (1, 4), (2, 2))),
        "reward_grad": gaussian(splits[1], (FRAMES, HEIGHT, WIDTH, C), 1.0, 6.0, ((0, 4), (1, 4), (2, 2))),
        "first_kernel": gaussian(splits[2], (3, 3, 3, C, C), (27 * C) ** -0.5, 0.0625, ((3, 4),)),
        "second_kernel": gaussian(splits[3], (3, 3, 3, C, C), (27 * C) ** -0.5, 0.0625, ((3, 4),)),
        "first_gain": jnp.clip(1.0 + 0.15 * jax.random.normal(splits[4], (C,), jnp.float32), 0.25, 1.75),
        "second_gain": jnp.clip(1.0 + 0.15 * jax.random.normal(splits[5], (C,), jnp.float32), 0.25, 1.75),
        "first_bias": gaussian(splits[6], (C,), 0.5, 3.0, (), jnp.float32),
    }


epsilon = 1e-06

def rms_parts(values, gain):
    inv_rms = lax.rsqrt(lax.optimization_barrier(jnp.mean(values * values, axis=-1, keepdims=True)) + epsilon)
    normed = values * inv_rms
    return (inv_rms, normed, normed * gain)

def silu_slope(values):
    sigmoid_val = jax.nn.sigmoid(values)
    return sigmoid_val * (1.0 + values * (1.0 - sigmoid_val))

def rms_back(cotangent, inv_rms, normed, gain):
    scaled_grad = cotangent * gain
    return inv_rms * (scaled_grad - normed * lax.optimization_barrier(jnp.mean(normed * scaled_grad, axis=-1, keepdims=True)))

def conv_causal(source, kernel):
    frame_count, row_count, col_count, channels = source.shape
    padded = jnp.pad(source, ((2, 0), (1, 1), (1, 1), (0, 0)))
    summed = jnp.zeros((frame_count * row_count * col_count, kernel.shape[4]), jnp.float32)
    for step_t in range(3):
        for step_h in range(3):
            for step_w in range(3):
                window = padded[step_t:step_t + frame_count, step_h:step_h + row_count, step_w:step_w + col_count]
                summed = summed + jnp.dot(window.reshape(-1, channels), kernel[step_t, step_h, step_w], preferred_element_type=jnp.float32)
    return summed

def conv_transposed(source, kernel):
    frame_count, row_count, col_count, channels = source.shape
    padded = jnp.pad(source, ((0, 2), (1, 1), (1, 1), (0, 0)))
    summed = jnp.zeros((frame_count * row_count * col_count, kernel.shape[3]), jnp.float32)
    for step_t in range(3):
        for step_h in range(3):
            for step_w in range(3):
                window = padded[2 - step_t:2 - step_t + frame_count, 2 - step_h:2 - step_h + row_count, 2 - step_w:2 - step_w + col_count]
                summed = summed + jnp.dot(window.reshape(-1, channels), kernel[step_t, step_h, step_w].T, preferred_element_type=jnp.float32)
    return summed

def reference(features, reward_grad, first_kernel, second_kernel, first_gain, second_gain, first_bias):
    frame_count, row_count, col_count, channels = features.shape
    flat_in = features.reshape(-1, channels).astype(jnp.float32)
    inv_one, normed_one, act_one = rms_parts(flat_in, first_gain)
    first_silu = jax.nn.silu(act_one).astype(jnp.bfloat16).reshape(features.shape)
    hidden = conv_causal(first_silu, first_kernel) + first_bias
    inv_two, normed_two, act_two = rms_parts(hidden, second_gain)
    second_back = conv_transposed(reward_grad, second_kernel)
    hidden_grad = rms_back(second_back * silu_slope(act_two), inv_two, normed_two, second_gain).astype(jnp.bfloat16)
    first_back = conv_transposed(hidden_grad.reshape(features.shape), first_kernel)
    result = rms_back(first_back * silu_slope(act_one), inv_one, normed_one, first_gain)
    result = result + reward_grad.reshape(-1, channels).astype(jnp.float32)
    return result.astype(jnp.bfloat16).reshape(features.shape)
```

```python
import functools

import jax
import jax.numpy as jnp
from jax import lax
from jax.experimental import pallas as pl
from jax.experimental.pallas import tpu as pltpu
from jax.sharding import PartitionSpec as P

epsilon = 1e-06
f32 = jnp.float32
bf16 = jnp.bfloat16
lanes = 128


def is_power(count):
    return count & (count - 1) == 0


def sent_to(index, step, count):
    return index ^ step if is_power(count) else lax.rem(index + step, count)


def got_from(index, step, count):
    return index ^ step if is_power(count) else lax.rem(index + count - step, count)


def tm_exchange(blocks):
    count = len(blocks)
    got = [blocks[0]]
    for step in range(1, count):
        pairs = [
            (i, i ^ step if is_power(count) else (i + step) % count) for i in range(count)
        ]
        got.append(lax.ppermute(blocks[step], "tm", pairs))
    return got


def halo_pair(low_edge, high_edge, axis):
    count = lax.axis_size(axis)
    if count == 1:
        return jnp.zeros_like(high_edge), jnp.zeros_like(low_edge)
    even = lax.axis_index(axis) % 2 == 0
    first = [(i, i + 1) for i in range(0, count - 1, 2)]
    second = [(i, i + 1) for i in range(1, count - 1, 2)]
    swap = lambda pairs: [(a, b) for a, b in pairs] + [(b, a) for a, b in pairs]
    in_first = lax.ppermute(jnp.where(even, high_edge, low_edge), axis, swap(first))
    if second:
        in_second = lax.ppermute(jnp.where(even, low_edge, high_edge), axis, swap(second))
    else:
        in_second = jnp.zeros_like(in_first)
    return jnp.where(even, in_second, in_first), jnp.where(even, in_first, in_second)


def with_halo(cells):
    row_dim, col_dim = cells.ndim - 3, cells.ndim - 2
    for axis, dim in (("col", col_dim), ("row", row_dim)):
        size = cells.shape[dim]
        low, high = halo_pair(
            lax.slice_in_dim(cells, 0, 1, axis=dim),
            lax.slice_in_dim(cells, size - 1, size, axis=dim),
            axis,
        )
        cells = jnp.concatenate([low, cells, high], axis=dim)
    return cells.reshape(cells.shape[:row_dim] + (-1, cells.shape[-1]))


def rms_parts(values, gain):
    inv_rms = lax.rsqrt(jnp.mean(values * values, axis=-1, keepdims=True) + epsilon)
    normed = values * inv_rms
    return inv_rms, normed, normed * gain


def silu_slope(values):
    sigmoid_val = jax.nn.sigmoid(values)
    return sigmoid_val * (1.0 + values * (1.0 - sigmoid_val))


def rms_back(cotangent, inv_rms, normed, gain):
    scaled_grad = cotangent * gain
    return inv_rms * (scaled_grad - normed * jnp.mean(normed * scaled_grad, axis=-1, keepdims=True))


def slot_matrix(slot, width, channels, wide):
    row = lax.broadcasted_iota(jnp.int32, (channels, wide), 0)
    col = lax.broadcasted_iota(jnp.int32, (channels, wide), 1)
    hit = (row == col + slot * width) & (col < width)
    return jnp.where(hit, 1.0, 0.0).astype(bf16)


def spread_matrix(slot, width, channels, wide):
    row = lax.broadcasted_iota(jnp.int32, (wide, channels), 0)
    col = lax.broadcasted_iota(jnp.int32, (wide, channels), 1)
    hit = (col == row + slot * width) & (row < width)
    return jnp.where(hit, 1.0, 0.0).astype(bf16)


def pack_kernel(peers, width, feat_ref, reward_ref, gain_ref, *out_refs):
    me = lax.axis_index("tm")
    frames, _, channels = feat_ref.shape
    wide = out_refs[0].shape[2] - channels
    for frame in range(frames):
        values = feat_ref[frame].astype(f32)
        act = rms_parts(values, gain_ref[...])[2]
        silu = (act * jax.nn.sigmoid(act)).astype(bf16)
        for step in range(peers):
            slot = sent_to(me, step, peers)
            piece = jnp.dot(
                silu, slot_matrix(slot, width, channels, wide), preferred_element_type=f32
            )
            out_refs[step][frame, :, :channels] = reward_ref[frame]
            out_refs[step][frame, :, channels:] = piece.astype(bf16)


def lay_frames(peers, frames, block_refs, cells_ref):
    me = lax.axis_index("tm")
    total = peers * frames
    for step in range(peers):
        source = got_from(me, step, peers)
        for frame in range(frames):
            for tile in range(cells_ref.shape[0]):
                piece = block_refs[step][frame, :, tile * lanes : (tile + 1) * lanes]
                place = pl.ds(source * frames + frame, piece.shape[0], stride=total)
                cells_ref[tile, place, :] = piece.astype(f32)


def shifted(values, ahead):
    total = values.shape[1]
    if ahead == 0:
        return values
    frame = lax.broadcasted_iota(jnp.int32, values.shape, 1)
    moved = pltpu.roll(values, (-ahead) % total, 1)
    keep = frame < total - ahead if ahead > 0 else frame >= -ahead
    return jnp.where(keep, moved, 0.0)


def lay_taps(cells_ref, taps_ref, first, count, total, aheads):
    plane_rows = taps_ref.shape[0]
    cols = taps_ref.shape[1] // total
    span = (cols + 2) * total

    @pl.loop(0, plane_rows)
    def _(row):
        base = pl.multiple_of(row * span, total)
        for tile in range(count):
            values = cells_ref[first + tile, pl.ds(base, span), :]
            values = values.reshape(cols + 2, total, lanes)
            for at, ahead in enumerate(aheads):
                moved = shifted(values, ahead)
                for step_w in range(3):
                    k = ((at * 3 + step_w) * count + tile) * lanes
                    taps_ref[row, :, k : k + lanes] = (
                        moved[step_w : step_w + cols].reshape(cols * total, lanes).astype(bf16)
                    )


def conv_rows(taps_ref, weight_ref, rows):
    summed = None
    for step_h in range(3):
        left = taps_ref[step_h : step_h + rows].reshape(-1, taps_ref.shape[2])
        part = jnp.dot(left, weight_ref[step_h], preferred_element_type=f32)
        summed = part if summed is None else summed + part
    return summed


def hand_out(peers, frames, total, sum_ref, out_refs, start):
    me = lax.axis_index("tm")
    for step in range(peers):
        target = sent_to(me, step, peers)
        for frame in range(frames):
            place = pl.ds(target * frames + frame, out_refs[step].shape[1], stride=total)
            for tile in range(sum_ref.shape[0]):
                at = start + tile * lanes
                out_refs[step][frame, :, at : at + lanes] = sum_ref[tile, place, :].astype(bf16)


def put(sum_ref, values):
    for tile in range(sum_ref.shape[0]):
        sum_ref[tile] = values[:, tile * lanes : (tile + 1) * lanes]


def both_kernel(peers, frames, rows, channels, *refs):
    blocks = refs[:peers]
    weight_one, weight_two = refs[peers : peers + 2]
    outs = refs[peers + 2 : 2 * peers + 2]
    cells, taps_silu, taps_reward, sum_one, sum_two = refs[2 * peers + 2 :]
    total = peers * frames
    lay_frames(peers, frames, blocks, cells)
    tiles = channels // lanes
    lay_taps(cells, taps_silu, tiles, cells.shape[0] - tiles, total, (-2, -1, 0))
    put(sum_one, conv_rows(taps_silu, weight_one, rows))
    hand_out(peers, frames, total, sum_one, outs, 0)
    lay_taps(cells, taps_reward, 0, tiles, total, (0, 1, 2))
    put(sum_two, conv_rows(taps_reward, weight_two, rows))
    hand_out(peers, frames, total, sum_two, outs, channels)


def back_kernel(peers, frames, rows, *refs):
    blocks = refs[:peers]
    weight = refs[peers]
    outs = refs[peers + 1 : 2 * peers + 1]
    cells, taps, sums = refs[2 * peers + 1 :]
    total = peers * frames
    lay_frames(peers, frames, blocks, cells)
    lay_taps(cells, taps, 0, cells.shape[0], total, (0, 1, 2))
    put(sums, conv_rows(taps, weight, rows))
    hand_out(peers, frames, total, sums, outs, 0)


def gathered(peers, frame, block_refs, start, width, channels):
    me = lax.axis_index("tm")
    wide = block_refs[0].shape[2] - start
    summed = None
    for step in range(peers):
        spread = spread_matrix(got_from(me, step, peers), width, channels, wide)
        part = jnp.dot(
            block_refs[step][frame, :, start:], spread, preferred_element_type=f32
        )
        summed = part if summed is None else summed + part
    return summed


def middle_kernel(peers, width, *refs):
    blocks = refs[:peers]
    gain_ref, bias_ref, out_ref = refs[peers:]
    frames, _, channels = out_ref.shape
    for frame in range(frames):
        hidden = blocks[0][frame, :, :channels].astype(f32)
        for step in range(1, peers):
            hidden = hidden + blocks[step][frame, :, :channels].astype(f32)
        hidden = hidden + bias_ref[...]
        back = gathered(peers, frame, blocks, channels, width, channels)
        inv, normed, act = rms_parts(hidden, gain_ref[...])
        out_ref[frame] = rms_back(back * silu_slope(act), inv, normed, gain_ref[...]).astype(bf16)


def final_kernel(peers, width, *refs):
    blocks = refs[:peers]
    feat_ref, reward_ref, gain_ref, out_ref = refs[peers:]
    frames, _, channels = out_ref.shape
    for frame in range(frames):
        back = gathered(peers, frame, blocks, 0, width, channels)
        inv, normed, act = rms_parts(feat_ref[frame].astype(f32), gain_ref[...])
        result = rms_back(back * silu_slope(act), inv, normed, gain_ref[...])
        out_ref[frame] = (result + reward_ref[frame].astype(f32)).astype(bf16)


def call(kernel, outs, scratch=(), flops=0, name=None):
    moved = sum(s.size * s.dtype.itemsize for s in outs)
    return pl.pallas_call(
        kernel,
        out_shape=outs,
        scratch_shapes=list(scratch),
        cost_estimate=pl.CostEstimate(flops=flops, bytes_accessed=moved, transcendentals=0),
        name=name,
    )


def on_device(
    features, reward_grad, first_kernel, second_kernel, first_gain, second_gain, first_bias
):
    peers = lax.axis_size("tm")
    frames, rows, cols, channels = features.shape
    width = first_kernel.shape[3]
    wide = -(-width // lanes) * lanes
    total = peers * frames
    plane = (rows + 2) * (cols + 2)
    count = rows * cols
    struct = jax.ShapeDtypeStruct
    gain_one, gain_two = first_gain[None], second_gain[None]

    def turned(kernel):
        kernel = kernel[::-1, ::-1, ::-1].transpose(1, 0, 2, 4, 3)
        kernel = jnp.pad(kernel, ((0, 0),) * 4 + ((0, wide - width),))
        return kernel.reshape(3, 9 * channels, wide)

    weight_one = jnp.pad(
        first_kernel.transpose(1, 0, 2, 3, 4), ((0, 0),) * 3 + ((0, wide - width), (0, 0))
    ).reshape(3, 9 * wide, channels)
    weight_two = turned(second_kernel)
    weight_back = turned(first_kernel)

    planes = with_halo(jnp.stack([features, reward_grad]))
    packed = call(
        functools.partial(pack_kernel, peers, width),
        [struct((frames, plane, channels + wide), bf16)] * peers,
        name="pack",
    )(planes[0], planes[1], gain_one)
    got = tm_exchange(packed)
    flops = 2 * 27 * width * channels * total * count
    sums = call(
        functools.partial(both_kernel, peers, frames, rows, channels),
        [struct((frames, count, channels + wide), bf16)] * peers,
        [
            pltpu.VMEM(((channels + wide) // lanes, plane * total, lanes), f32),
            pltpu.VMEM((rows + 2, cols * total, 9 * wide), bf16),
            pltpu.VMEM((rows + 2, cols * total, 9 * channels), bf16),
            pltpu.VMEM((channels // lanes, count * total, lanes), f32),
            pltpu.VMEM((wide // lanes, count * total, lanes), f32),
        ],
        2 * flops,
        name="both",
    )(*got, weight_one, weight_two)
    got = tm_exchange(sums)
    hidden_grad = call(
        functools.partial(middle_kernel, peers, width),
        [struct((frames, count, channels), bf16)],
        name="middle",
    )(*got, gain_two, first_bias[None])[0]
    hidden_plane = with_halo(hidden_grad.reshape(features.shape))
    got = tm_exchange([hidden_plane] * peers)
    backs = call(
        functools.partial(back_kernel, peers, frames, rows),
        [struct((frames, count, wide), bf16)] * peers,
        [
            pltpu.VMEM((channels // lanes, plane * total, lanes), f32),
            pltpu.VMEM((rows + 2, cols * total, 9 * channels), bf16),
            pltpu.VMEM((wide // lanes, count * total, lanes), f32),
        ],
        flops,
        name="back",
    )(*got, weight_back)
    got = tm_exchange(backs)
    flat = (frames, count, channels)
    result = call(
        functools.partial(final_kernel, peers, width), [struct(flat, bf16)], name="final"
    )(*got, features.reshape(flat), reward_grad.reshape(flat), gain_one)[0]
    return result.reshape(features.shape)


def solution(mesh):
    in_specs = (
        P("tm", "row", "col", None),
        P("tm", "row", "col", None),
        P(None, None, None, "tm", None),
        P(None, None, None, "tm", None),
        P(),
        P(),
        P(),
    )
    out_specs = P("tm", "row", "col", None)
    return jax.shard_map(
        on_device, mesh=mesh, in_specs=in_specs, out_specs=out_specs, check_vma=False
    )
```

```python
import functools
import math

import jax
import jax.numpy as jnp
from jax import lax
from jax.experimental import pallas as pl
from jax.experimental.pallas import tpu as pltpu
from jax.sharding import PartitionSpec as P

epsilon = 1e-06
f32 = jnp.float32
bf16 = jnp.bfloat16
lanes = 128


def is_power(count):
    return count & (count - 1) == 0


def sent_to(index, step, count):
    return index ^ step if is_power(count) else lax.rem(index + step, count)


def got_from(index, step, count):
    return index ^ step if is_power(count) else lax.rem(index + count - step, count)


def tm_exchange(blocks):
    count = len(blocks)
    got = [blocks[0]]
    for step in range(1, count):
        pairs = [
            (i, i ^ step if is_power(count) else (i + step) % count) for i in range(count)
        ]
        got.append(lax.ppermute(blocks[step], "tm", pairs))
    return got


def is_even(axis):
    return lax.rem(lax.axis_index(axis), 2) == 0


def halo_swaps(low_edge, high_edge, axis):
    count = lax.axis_size(axis)
    even = is_even(axis)
    got = []
    for start, value in ((0, (high_edge, low_edge)), (1, (low_edge, high_edge))):
        pairs = [(i, i + 1) for i in range(start, count - 1, 2)]
        if pairs:
            pairs = pairs + [(b, a) for a, b in pairs]
            got.append(lax.ppermute(jnp.where(even, *value), axis, pairs))
        else:
            got.append(None)
    return got


def low_and_high(axis, first, second):
    even = is_even(axis)
    if first is None:
        return None, None
    nothing = jnp.zeros_like(first)
    second = nothing if second is None else second
    return jnp.where(even, second, first), jnp.where(even, first, second)


def edges(cells, dim):
    size = cells.shape[dim]
    return (
        lax.slice_in_dim(cells, 0, 1, axis=dim),
        lax.slice_in_dim(cells, size - 1, size, axis=dim),
    )


def joined(low, cells, high, dim):
    if low is None:
        low = high = jnp.zeros_like(edges(cells, dim)[0])
    return jnp.concatenate([low, cells, high], axis=dim)


def with_halo(cells, axis, dim):
    got = halo_swaps(*edges(cells, dim), axis)
    low, high = low_and_high(axis, *got)
    return joined(low, cells, high, dim)


def rms_parts(values, gain):
    inv_rms = lax.rsqrt(jnp.mean(values * values, axis=-1, keepdims=True) + epsilon)
    normed = values * inv_rms
    return inv_rms, normed, normed * gain


def silu_slope(values):
    sigmoid_val = jax.nn.sigmoid(values)
    return sigmoid_val * (1.0 + values * (1.0 - sigmoid_val))


def rms_back(cotangent, inv_rms, normed, gain):
    scaled_grad = cotangent * gain
    return inv_rms * (scaled_grad - normed * jnp.mean(normed * scaled_grad, axis=-1, keepdims=True))


def slot_matrix(slot, width, channels, wide):
    row = lax.broadcasted_iota(jnp.int32, (channels, wide), 0)
    col = lax.broadcasted_iota(jnp.int32, (channels, wide), 1)
    hit = (row == col + slot * width) & (col < width)
    return jnp.where(hit, 1.0, 0.0).astype(bf16)


def spread_matrix(slot, width, channels, wide):
    row = lax.broadcasted_iota(jnp.int32, (wide, channels), 0)
    col = lax.broadcasted_iota(jnp.int32, (wide, channels), 1)
    hit = (col == row + slot * width) & (row < width)
    return jnp.where(hit, 1.0, 0.0).astype(bf16)


def pack_kernel(peers, width, *refs):
    strips_ref, *edge_refs = refs[: -peers - 2]
    gain_ref, *out_refs = refs[-peers - 2 : -1]
    plane_ref = refs[-1]
    me = lax.axis_index("tm")
    _, frames, rows, span, channels = strips_ref.shape
    wide = out_refs[0].shape[2] - channels
    for frame in range(frames):
        for array in range(2):
            got = [ref[array, frame, 0].astype(f32) for ref in edge_refs] + [None, None]
            low, high = low_and_high("row", got[0], got[1])
            if low is None:
                low = high = jnp.zeros((span, channels), f32)
            strips = [strips_ref[array, frame, row].astype(f32) for row in range(rows)]
            for row, strip in enumerate([low, *strips, high]):
                plane_ref[array, row * span : (row + 1) * span, :] = strip
        act = rms_parts(plane_ref[0], gain_ref[...])[2]
        silu = (act * jax.nn.sigmoid(act)).astype(bf16)
        reward = plane_ref[1].astype(bf16)
        for step in range(peers):
            slot = sent_to(me, step, peers)
            piece = jnp.dot(
                silu, slot_matrix(slot, width, channels, wide), preferred_element_type=f32
            )
            out_refs[step][frame, :, :channels] = reward
            out_refs[step][frame, :, channels:] = piece.astype(bf16)


def lay_frames(peers, frames, block_refs, cells_ref):
    me = lax.axis_index("tm")
    total = peers * frames
    for step in range(peers):
        source = got_from(me, step, peers)
        for frame in range(frames):
            for tile in range(cells_ref.shape[0]):
                piece = block_refs[step][frame, :, tile * lanes : (tile + 1) * lanes]
                place = pl.ds(source * frames + frame, piece.shape[0], stride=total)
                cells_ref[tile, place, :] = piece.astype(f32)


def shifted(values, ahead):
    total = values.shape[1]
    if ahead == 0:
        return values
    frame = lax.broadcasted_iota(jnp.int32, values.shape, 1)
    moved = pltpu.roll(values, (-ahead) % total, 1)
    keep = frame < total - ahead if ahead > 0 else frame >= -ahead
    return jnp.where(keep, moved, 0.0)


def chunk_rows(rows, total):
    return max(r for r in range(1, rows + 1) if rows % r == 0 and (r == 1 or r * total <= 32))


def stacked_weights(kernel_ref, wide, order):
    width, channels = kernel_ref.shape[3:]
    pad = jnp.zeros((wide - width, channels), bf16)

    def block(a, b, c):
        value = kernel_ref[a, b, c]
        return jnp.concatenate([value, pad], axis=0) if wide > width else value

    return jnp.concatenate(
        [jnp.concatenate([block(*tap) for tap in column], axis=0) for column in order], axis=1
    )


def conv_ahead(
    cells_ref, first, kernel_ref, plane_ref, parts_ref, sum_ref, rows, total, cols_first=False
):
    plane_rows, span, channels = plane_ref.shape
    cols = span // total - 2
    wide = sum_ref.shape[0] * lanes
    wide_tiles = wide // lanes

    @pl.loop(0, plane_rows)
    def _(row):
        base = pl.multiple_of(row * span, total)
        for tile in range(channels // lanes):
            plane_ref[row, :, tile * lanes : (tile + 1) * lanes] = cells_ref[
                first + tile, pl.ds(base, span), :
            ].astype(bf16)

    weights = stacked_weights(
        kernel_ref,
        wide,
        [[(2 - s, 2 - b, 2 - c) for s in range(3) for c in range(3)] for b in range(3)],
    )
    step = chunk_rows(rows, total)

    def chunk(start):
        left = jnp.concatenate(
            [plane_ref[pl.ds(start + b, step)].reshape(-1, channels) for b in range(3)], axis=1
        )
        parts = lax.dot_general(left, weights, (((1,), (1,)), ((), ())), preferred_element_type=f32)
        for tile in range(parts_ref.shape[0]):
            parts_ref[tile] = parts[:, tile * lanes : (tile + 1) * lanes]
        for row in range(step):
            for tile in range(wide_tiles):
                summed = None
                for s in range(3):
                    part = None
                    for c in range(3):
                        at = (row * (cols + 2) + c) * total
                        piece = parts_ref[(s * 3 + c) * wide_tiles + tile, at : at + cols * total, :]
                        part = piece if part is None else part + piece
                    part = shifted(part.reshape(cols, total, lanes), s)
                    summed = part if summed is None else summed + part
                if cols_first:
                    for col in range(cols):
                        place = pl.ds((col * rows + start + row) * total, total)
                        sum_ref[tile, place, :] = summed[col]
                else:
                    place = pl.ds((start + row) * cols * total, cols * total)
                    sum_ref[tile, place, :] = summed.reshape(cols * total, lanes)

    run_chunks(rows, step, chunk)


def run_chunks(rows, step, chunk):
    if step == rows:
        chunk(0)
    else:
        pl.loop(0, rows, step=step)(chunk)


def conv_behind(cells_ref, first, kernel_ref, taps_ref, sum_ref, rows, total):
    plane_rows, cols = taps_ref.shape[0], taps_ref.shape[1] // total
    channels = sum_ref.shape[0] * lanes
    wide_tiles = taps_ref.shape[2] // (3 * lanes)
    span = (cols + 2) * total

    @pl.loop(0, plane_rows)
    def _(row):
        base = pl.multiple_of(row * span, total)
        for tile in range(wide_tiles):
            for c in range(3):
                at = (c * wide_tiles + tile) * lanes
                taps_ref[row, :, at : at + lanes] = cells_ref[
                    first + tile, pl.ds(base + c * total, cols * total), :
                ].astype(bf16)

    weights = stacked_weights(
        kernel_ref,
        wide_tiles * lanes,
        [[(a, b, c) for b in range(3) for c in range(3)] for a in range(3)],
    )
    step = chunk_rows(rows, total)

    def chunk(start):
        left = jnp.concatenate(
            [
                taps_ref[pl.ds(start + b, step)].reshape(-1, taps_ref.shape[2])
                for b in range(3)
            ],
            axis=1,
        )
        parts = jnp.dot(left, weights, preferred_element_type=f32)
        place = pl.ds(start * cols * total, step * cols * total)
        for tile in range(channels // lanes):
            summed = None
            for a in range(3):
                at = a * channels + tile * lanes
                part = parts[:, at : at + lanes].reshape(step * cols, total, lanes)
                part = shifted(part, a - 2)
                summed = part if summed is None else summed + part
            sum_ref[tile, place, :] = summed.reshape(-1, lanes)

    run_chunks(rows, step, chunk)


def hand_out(peers, frames, total, sum_ref, out_refs, start):
    me = lax.axis_index("tm")
    for step in range(peers):
        target = sent_to(me, step, peers)
        for frame in range(frames):
            place = pl.ds(target * frames + frame, out_refs[step].shape[1], stride=total)
            for tile in range(sum_ref.shape[0]):
                at = start + tile * lanes
                out_refs[step][frame, :, at : at + lanes] = sum_ref[tile, place, :].astype(bf16)


def both_kernel(peers, frames, rows, channels, *refs):
    blocks = refs[:peers]
    kernel_one, kernel_two = refs[peers : peers + 2]
    outs = refs[peers + 2 : 2 * peers + 2]
    cells, taps, plane, parts, sum_one, sum_two = refs[2 * peers + 2 :]
    total = peers * frames
    tiles = channels // lanes
    lay_frames(peers, frames, blocks, cells)
    conv_behind(cells, tiles, kernel_one, taps, sum_one, rows, total)
    hand_out(peers, frames, total, sum_one, outs, 0)
    conv_ahead(cells, 0, kernel_two, plane, parts, sum_two, rows, total)
    hand_out(peers, frames, total, sum_two, outs, channels)


def back_kernel(peers, frames, rows, *refs):
    blocks = refs[:peers]
    kernel = refs[peers]
    outs = refs[peers + 1 : 2 * peers + 1]
    cells, plane, parts, sums = refs[2 * peers + 1 :]
    total = peers * frames
    lay_frames(peers, frames, blocks, cells)
    conv_ahead(cells, 0, kernel, plane, parts, sums, rows, total, cols_first=True)
    hand_out(peers, frames, total, sums, outs, 0)


def gathered(peers, frame, block_refs, start, width, channels):
    me = lax.axis_index("tm")
    wide = block_refs[0].shape[2] - start
    summed = None
    for step in range(peers):
        spread = spread_matrix(got_from(me, step, peers), width, channels, wide)
        part = jnp.dot(
            block_refs[step][frame, :, start:], spread, preferred_element_type=f32
        )
        summed = part if summed is None else summed + part
    return summed


def split_rows(flat_ref, values, out_ref, frame):
    flat_ref[...] = values
    cols = out_ref.shape[2]
    for row in range(out_ref.shape[1]):
        out_ref[frame, row] = flat_ref[row * cols : (row + 1) * cols, :].astype(bf16)


def join_rows(flat_ref, in_ref, frame):
    cols = in_ref.shape[2]
    for row in range(in_ref.shape[1]):
        flat_ref[row * cols : (row + 1) * cols, :] = in_ref[frame, row].astype(f32)
    return flat_ref[...]


def middle_kernel(peers, width, *refs):
    blocks = refs[:peers]
    gain_ref, bias_ref, out_ref, flat_ref = refs[peers:]
    frames, channels = out_ref.shape[0], out_ref.shape[3]
    for frame in range(frames):
        hidden = blocks[0][frame, :, :channels].astype(f32)
        for step in range(1, peers):
            hidden = hidden + blocks[step][frame, :, :channels].astype(f32)
        hidden = hidden + bias_ref[...]
        back = gathered(peers, frame, blocks, channels, width, channels)
        inv, normed, act = rms_parts(hidden, gain_ref[...])
        grad = rms_back(back * silu_slope(act), inv, normed, gain_ref[...])
        split_rows(flat_ref.at[frame], grad, out_ref, frame)


def final_kernel(peers, width, *refs):
    blocks = refs[:peers]
    feat_ref, reward_ref, gain_ref, out_ref, flat_ref = refs[peers:]
    frames, channels = out_ref.shape[0], out_ref.shape[3]
    for frame in range(frames):
        back = gathered(peers, frame, blocks, 0, width, channels)
        cells = join_rows(flat_ref.at[frame, 0], feat_ref, frame)
        reward = join_rows(flat_ref.at[frame, 1], reward_ref, frame)
        inv, normed, act = rms_parts(cells, gain_ref[...])
        result = rms_back(back * silu_slope(act), inv, normed, gain_ref[...])
        split_rows(flat_ref.at[frame, 2], result + reward, out_ref, frame)


def size_of(structs):
    return sum(math.prod(s.shape) * s.dtype.itemsize for s in structs)


def call(kernel, outs, scratch=(), flops=0, spare=2, name=None):
    def run(*operands):
        held = size_of(outs) + size_of(operands)
        grant = 2 * held + size_of(scratch) + spare * 2**20
        return pl.pallas_call(
            kernel,
            out_shape=outs,
            scratch_shapes=list(scratch),
            cost_estimate=pl.CostEstimate(
                flops=flops, bytes_accessed=held, transcendentals=0
            ),
            compiler_params=pltpu.CompilerParams(vmem_limit_bytes=min(grant, 60 * 2**20)),
            name=name,
        )(*operands)

    return run


def on_device(
    features, reward_grad, first_kernel, second_kernel, first_gain, second_gain, first_bias
):
    peers = lax.axis_size("tm")
    frames, rows, cols, channels = features.shape
    width = first_kernel.shape[3]
    wide = -(-width // lanes) * lanes
    total = peers * frames
    plane = (rows + 2) * (cols + 2)
    count = rows * cols
    struct = jax.ShapeDtypeStruct
    gain_one, gain_two = first_gain[None], second_gain[None]

    strips = with_halo(jnp.stack([features, reward_grad]), "col", 3)
    row_edges = [got for got in halo_swaps(*edges(strips, 2), "row") if got is not None]
    packed = call(
        functools.partial(pack_kernel, peers, width),
        [struct((frames, plane, channels + wide), bf16)] * peers,
        [pltpu.VMEM((2, plane, channels), f32)],
        name="pack",
    )(strips, *row_edges, gain_one)
    got = tm_exchange(packed)
    ahead_scratch = [
        pltpu.VMEM((rows + 2, (cols + 2) * total, channels), bf16),
        pltpu.VMEM((9 * wide // lanes, chunk_rows(rows, total) * (cols + 2) * total, lanes), f32),
    ]
    flops = 2 * 27 * width * channels * total * count
    sums = call(
        functools.partial(both_kernel, peers, frames, rows, channels),
        [struct((frames, count, channels + wide), bf16)] * peers,
        [
            pltpu.VMEM(((channels + wide) // lanes, plane * total, lanes), f32),
            pltpu.VMEM((rows + 2, cols * total, 3 * wide), bf16),
            *ahead_scratch,
            pltpu.VMEM((channels // lanes, count * total, lanes), f32),
            pltpu.VMEM((wide // lanes, count * total, lanes), f32),
        ],
        2 * flops,
        spare=8,
        name="both",
    )(*got, first_kernel, second_kernel)
    got = tm_exchange(sums)
    hidden_grad = call(
        functools.partial(middle_kernel, peers, width),
        [struct(features.shape, bf16)],
        [pltpu.VMEM((frames, count, channels), f32)],
        name="middle",
    )(*got, gain_two, first_bias[None])[0]
    hidden_plane = with_halo(with_halo(hidden_grad, "col", 2), "row", 1)
    got = tm_exchange([hidden_plane.reshape(frames, plane, channels)] * peers)
    backs = call(
        functools.partial(back_kernel, peers, frames, rows),
        [struct((frames, count, wide), bf16)] * peers,
        [
            pltpu.VMEM((channels // lanes, plane * total, lanes), f32),
            *ahead_scratch,
            pltpu.VMEM((wide // lanes, count * total, lanes), f32),
        ],
        flops,
        spare=8,
        name="back",
    )(*got, first_kernel)
    got = tm_exchange(backs)
    by_col = (0, 2, 1, 3)
    held = features.transpose(by_col), reward_grad.transpose(by_col)
    result = call(
        functools.partial(final_kernel, peers, width),
        [struct(held[0].shape, bf16)],
        [pltpu.VMEM((frames, 3, count, channels), f32)],
        name="final",
    )(*got, *held, gain_one)[0]
    return result.transpose(by_col)


def solution(mesh):
    in_specs = (
        P("tm", "row", "col", None),
        P("tm", "row", "col", None),
        P(None, None, None, "tm", None),
        P(None, None, None, "tm", None),
        P(),
        P(),
        P(),
    )
    out_specs = P("tm", "row", "col", None)
    return jax.shard_map(
        on_device, mesh=mesh, in_specs=in_specs, out_specs=out_specs, check_vma=False
    )
```

```python
import functools
import math

import jax
import jax.numpy as jnp
from jax import lax
from jax.experimental import pallas as pl
from jax.experimental.pallas import tpu as pltpu
from jax.sharding import PartitionSpec as P

epsilon = 1e-06
f32 = jnp.float32
bf16 = jnp.bfloat16
lanes = 128


def is_power(count):
    return count & (count - 1) == 0


def sent_to(index, step, count):
    return index ^ step if is_power(count) else lax.rem(index + step, count)


def got_from(index, step, count):
    return index ^ step if is_power(count) else lax.rem(index + count - step, count)


def tm_exchange(blocks):
    count = len(blocks)
    got = [blocks[0]]
    for step in range(1, count):
        pairs = [
            (i, i ^ step if is_power(count) else (i + step) % count) for i in range(count)
        ]
        got.append(lax.ppermute(blocks[step], "tm", pairs))
    return got


def is_even(axis):
    return lax.rem(lax.axis_index(axis), 2) == 0


def halo_swaps(low_edge, high_edge, axis):
    count = lax.axis_size(axis)
    even = is_even(axis)
    got = []
    for start, value in ((0, (high_edge, low_edge)), (1, (low_edge, high_edge))):
        pairs = [(i, i + 1) for i in range(start, count - 1, 2)]
        if pairs:
            pairs = pairs + [(b, a) for a, b in pairs]
            got.append(lax.ppermute(jnp.where(even, *value), axis, pairs))
        else:
            got.append(None)
    return got


def low_and_high(axis, first, second):
    even = is_even(axis)
    if first is None:
        return None, None
    nothing = jnp.zeros_like(first)
    second = nothing if second is None else second
    return jnp.where(even, second, first), jnp.where(even, first, second)


def edges(cells, dim):
    size = cells.shape[dim]
    return (
        lax.slice_in_dim(cells, 0, 1, axis=dim),
        lax.slice_in_dim(cells, size - 1, size, axis=dim),
    )


def joined(low, cells, high, dim):
    if low is None:
        low = high = jnp.zeros_like(edges(cells, dim)[0])
    return jnp.concatenate([low, cells, high], axis=dim)


def with_halo(cells, axis, dim):
    got = halo_swaps(*edges(cells, dim), axis)
    low, high = low_and_high(axis, *got)
    return joined(low, cells, high, dim)


def rms_parts(values, gain):
    inv_rms = lax.rsqrt(jnp.mean(values * values, axis=-1, keepdims=True) + epsilon)
    normed = values * inv_rms
    return inv_rms, normed, normed * gain


def silu_slope(values):
    sigmoid_val = jax.nn.sigmoid(values)
    return sigmoid_val * (1.0 + values * (1.0 - sigmoid_val))


def rms_back(cotangent, inv_rms, normed, gain):
    scaled_grad = cotangent * gain
    return inv_rms * (scaled_grad - normed * jnp.mean(normed * scaled_grad, axis=-1, keepdims=True))


def slot_matrix(slot, width, channels, wide):
    row = lax.broadcasted_iota(jnp.int32, (channels, wide), 0)
    col = lax.broadcasted_iota(jnp.int32, (channels, wide), 1)
    hit = (row == col + slot * width) & (col < width)
    return jnp.where(hit, 1.0, 0.0).astype(bf16)


def spread_matrix(slot, width, channels, wide):
    row = lax.broadcasted_iota(jnp.int32, (wide, channels), 0)
    col = lax.broadcasted_iota(jnp.int32, (wide, channels), 1)
    hit = (col == row + slot * width) & (row < width)
    return jnp.where(hit, 1.0, 0.0).astype(bf16)


def pack_kernel(peers, width, *refs):
    strips_ref, *edge_refs = refs[: -peers - 2]
    gain_ref, *out_refs = refs[-peers - 2 : -1]
    plane_ref = refs[-1]
    me = lax.axis_index("tm")
    _, frames, rows, span, channels = strips_ref.shape
    wide = out_refs[0].shape[2] - channels
    for frame in range(frames):
        for array in range(2):
            got = [ref[array, frame, 0].astype(f32) for ref in edge_refs] + [None, None]
            low, high = low_and_high("row", got[0], got[1])
            if low is None:
                low = high = jnp.zeros((span, channels), f32)
            strips = [strips_ref[array, frame, row].astype(f32) for row in range(rows)]
            for row, strip in enumerate([low, *strips, high]):
                plane_ref[array, row * span : (row + 1) * span, :] = strip
        act = rms_parts(plane_ref[0], gain_ref[...])[2]
        silu = (act * jax.nn.sigmoid(act)).astype(bf16)
        reward = plane_ref[1].astype(bf16)
        for step in range(peers):
            slot = sent_to(me, step, peers)
            piece = jnp.dot(
                silu, slot_matrix(slot, width, channels, wide), preferred_element_type=f32
            )
            out_refs[step][frame, :, :channels] = reward
            out_refs[step][frame, :, channels:] = piece.astype(bf16)


def lay_frames(peers, frames, block_refs, cells_ref):
    me = lax.axis_index("tm")
    total = peers * frames
    for step in range(peers):
        source = got_from(me, step, peers)
        for frame in range(frames):
            for tile in range(cells_ref.shape[0]):
                piece = block_refs[step][frame, :, tile * lanes : (tile + 1) * lanes]
                place = pl.ds(source * frames + frame, piece.shape[0], stride=total)
                cells_ref[tile, place, :] = piece.astype(f32)


def shifted(values, ahead):
    total = values.shape[1]
    if ahead == 0:
        return values
    frame = lax.broadcasted_iota(jnp.int32, values.shape, 1)
    moved = pltpu.roll(values, (-ahead) % total, 1)
    keep = frame < total - ahead if ahead > 0 else frame >= -ahead
    return jnp.where(keep, moved, 0.0)


def chunk_rows(rows, total):
    return max(r for r in range(1, rows + 1) if rows % r == 0 and (r == 1 or r * total <= 32))


def stacked_weights(kernel_ref, wide, order):
    width, channels = kernel_ref.shape[3:]
    pad = jnp.zeros((wide - width, channels), bf16)

    def block(a, b, c):
        value = kernel_ref[a, b, c]
        return jnp.concatenate([value, pad], axis=0) if wide > width else value

    return jnp.concatenate(
        [jnp.concatenate([block(*tap) for tap in column], axis=0) for column in order], axis=1
    )


def conv_ahead(
    cells_ref, first, kernel_ref, plane_ref, parts_ref, sum_ref, rows, total, cols_first=False
):
    plane_rows, span, channels = plane_ref.shape
    cols = span // total - 2
    wide = sum_ref.shape[0] * lanes
    wide_tiles = wide // lanes

    @pl.loop(0, plane_rows)
    def _(row):
        base = pl.multiple_of(row * span, total)
        for tile in range(channels // lanes):
            plane_ref[row, :, tile * lanes : (tile + 1) * lanes] = cells_ref[
                first + tile, pl.ds(base, span), :
            ].astype(bf16)

    weights = stacked_weights(
        kernel_ref,
        wide,
        [[(2 - s, 2 - b, 2 - c) for s in range(3) for c in range(3)] for b in range(3)],
    )
    step = chunk_rows(rows, total)

    def chunk(start):
        left = jnp.concatenate(
            [plane_ref[pl.ds(start + b, step)].reshape(-1, channels) for b in range(3)], axis=1
        )
        parts = lax.dot_general(left, weights, (((1,), (1,)), ((), ())), preferred_element_type=f32)
        for tile in range(parts_ref.shape[0]):
            parts_ref[tile] = parts[:, tile * lanes : (tile + 1) * lanes]
        for row in range(step):
            for tile in range(wide_tiles):
                summed = None
                for s in range(3):
                    part = None
                    for c in range(3):
                        at = (row * (cols + 2) + c) * total
                        piece = parts_ref[(s * 3 + c) * wide_tiles + tile, at : at + cols * total, :]
                        part = piece if part is None else part + piece
                    part = shifted(part.reshape(cols, total, lanes), s)
                    summed = part if summed is None else summed + part
                if cols_first:
                    for col in range(cols):
                        place = pl.ds((col * rows + start + row) * total, total)
                        sum_ref[tile, place, :] = summed[col]
                else:
                    place = pl.ds((start + row) * cols * total, cols * total)
                    sum_ref[tile, place, :] = summed.reshape(cols * total, lanes)

    run_chunks(rows, step, chunk)


def run_chunks(rows, step, chunk):
    if step == rows:
        chunk(0)
    else:
        pl.loop(0, rows, step=step)(chunk)


def conv_behind(cells_ref, first, kernel_ref, taps_ref, sum_ref, rows, total):
    plane_rows, cols = taps_ref.shape[0], taps_ref.shape[1] // total
    channels = sum_ref.shape[0] * lanes
    wide_tiles = taps_ref.shape[2] // (3 * lanes)
    span = (cols + 2) * total

    @pl.loop(0, plane_rows)
    def _(row):
        base = pl.multiple_of(row * span, total)
        for tile in range(wide_tiles):
            for c in range(3):
                at = (c * wide_tiles + tile) * lanes
                taps_ref[row, :, at : at + lanes] = cells_ref[
                    first + tile, pl.ds(base + c * total, cols * total), :
                ].astype(bf16)

    weights = stacked_weights(
        kernel_ref,
        wide_tiles * lanes,
        [[(a, b, c) for b in range(3) for c in range(3)] for a in range(3)],
    )
    step = chunk_rows(rows, total)

    def chunk(start):
        left = jnp.concatenate(
            [
                taps_ref[pl.ds(start + b, step)].reshape(-1, taps_ref.shape[2])
                for b in range(3)
            ],
            axis=1,
        )
        parts = jnp.dot(left, weights, preferred_element_type=f32)
        place = pl.ds(start * cols * total, step * cols * total)
        for tile in range(channels // lanes):
            summed = None
            for a in range(3):
                at = a * channels + tile * lanes
                part = parts[:, at : at + lanes].reshape(step * cols, total, lanes)
                part = shifted(part, a - 2)
                summed = part if summed is None else summed + part
            sum_ref[tile, place, :] = summed.reshape(-1, lanes)

    run_chunks(rows, step, chunk)


def hand_out(peers, frames, total, sum_ref, out_refs, start):
    me = lax.axis_index("tm")
    for step in range(peers):
        target = sent_to(me, step, peers)
        for frame in range(frames):
            place = pl.ds(target * frames + frame, out_refs[step].shape[1], stride=total)
            for tile in range(sum_ref.shape[0]):
                at = start + tile * lanes
                out_refs[step][frame, :, at : at + lanes] = sum_ref[tile, place, :].astype(bf16)


def both_kernel(peers, frames, rows, channels, *refs):
    blocks = refs[:peers]
    kernel_one, kernel_two = refs[peers : peers + 2]
    outs = refs[peers + 2 : 2 * peers + 2]
    cells, taps, plane, parts, sum_one, sum_two = refs[2 * peers + 2 :]
    total = peers * frames
    tiles = channels // lanes
    lay_frames(peers, frames, blocks, cells)
    conv_behind(cells, tiles, kernel_one, taps, sum_one, rows, total)
    hand_out(peers, frames, total, sum_one, outs, 0)
    conv_ahead(cells, 0, kernel_two, plane, parts, sum_two, rows, total)
    hand_out(peers, frames, total, sum_two, outs, channels)


def back_kernel(peers, frames, rows, *refs):
    blocks = refs[:peers]
    kernel = refs[peers]
    outs = refs[peers + 1 : 2 * peers + 1]
    cells, plane, parts, sums = refs[2 * peers + 1 :]
    total = peers * frames
    lay_frames(peers, frames, blocks, cells)
    conv_ahead(cells, 0, kernel, plane, parts, sums, rows, total, cols_first=True)
    hand_out(peers, frames, total, sums, outs, 0)


def gathered(peers, frame, block_refs, start, width, channels):
    me = lax.axis_index("tm")
    wide = block_refs[0].shape[2] - start
    summed = None
    for step in range(peers):
        spread = spread_matrix(got_from(me, step, peers), width, channels, wide)
        part = jnp.dot(
            block_refs[step][frame, :, start:], spread, preferred_element_type=f32
        )
        summed = part if summed is None else summed + part
    return summed


def split_rows(flat_ref, values, out_ref, frame):
    flat_ref[...] = values
    cols = out_ref.shape[2]
    for row in range(out_ref.shape[1]):
        out_ref[frame, row] = flat_ref[row * cols : (row + 1) * cols, :].astype(bf16)


def join_rows(flat_ref, in_ref, frame):
    cols = in_ref.shape[2]
    for row in range(in_ref.shape[1]):
        flat_ref[row * cols : (row + 1) * cols, :] = in_ref[frame, row].astype(f32)
    return flat_ref[...]


def middle_kernel(peers, width, *refs):
    blocks = refs[:peers]
    gain_ref, bias_ref, out_ref, flat_ref = refs[peers:]
    frames, channels = out_ref.shape[0], out_ref.shape[3]
    for frame in range(frames):
        hidden = blocks[0][frame, :, :channels].astype(f32)
        for step in range(1, peers):
            hidden = hidden + blocks[step][frame, :, :channels].astype(f32)
        hidden = hidden + bias_ref[...]
        back = gathered(peers, frame, blocks, channels, width, channels)
        inv, normed, act = rms_parts(hidden, gain_ref[...])
        grad = rms_back(back * silu_slope(act), inv, normed, gain_ref[...])
        split_rows(flat_ref.at[frame], grad, out_ref, frame)


def final_kernel(peers, width, *refs):
    blocks = refs[:peers]
    feat_ref, reward_ref, gain_ref, out_ref, flat_ref = refs[peers:]
    frames, channels = out_ref.shape[0], out_ref.shape[3]
    for frame in range(frames):
        back = gathered(peers, frame, blocks, 0, width, channels)
        cells = join_rows(flat_ref.at[frame, 0], feat_ref, frame)
        reward = join_rows(flat_ref.at[frame, 1], reward_ref, frame)
        inv, normed, act = rms_parts(cells, gain_ref[...])
        result = rms_back(back * silu_slope(act), inv, normed, gain_ref[...])
        split_rows(flat_ref.at[frame, 2], result + reward, out_ref, frame)


def size_of(structs):
    return sum(math.prod(s.shape) * s.dtype.itemsize for s in structs)


def call(kernel, outs, scratch=(), flops=0, spare=2, covered=0, name=None):
    def run(*operands):
        held = size_of(outs) + size_of(operands)
        grant = 2 * held + size_of(scratch) + spare * 2**20
        return pl.pallas_call(
            kernel,
            out_shape=outs,
            scratch_shapes=list(scratch),
            cost_estimate=pl.CostEstimate(
                flops=flops + covered, bytes_accessed=held, transcendentals=0
            ),
            compiler_params=pltpu.CompilerParams(vmem_limit_bytes=min(grant, 60 * 2**20)),
            name=name,
        )(*operands)

    return run


def on_device(
    features, reward_grad, first_kernel, second_kernel, first_gain, second_gain, first_bias
):
    peers = lax.axis_size("tm")
    frames, rows, cols, channels = features.shape
    width = first_kernel.shape[3]
    wide = -(-width // lanes) * lanes
    total = peers * frames
    plane = (rows + 2) * (cols + 2)
    count = rows * cols
    struct = jax.ShapeDtypeStruct
    gain_one, gain_two = first_gain[None], second_gain[None]

    strips = with_halo(jnp.stack([features, reward_grad]), "col", 3)
    row_edges = [got for got in halo_swaps(*edges(strips, 2), "row") if got is not None]
    packed = call(
        functools.partial(pack_kernel, peers, width),
        [struct((frames, plane, channels + wide), bf16)] * peers,
        [pltpu.VMEM((2, plane, channels), f32)],
        covered=4 * 10**9,
        name="pack",
    )(strips, *row_edges, gain_one)
    got = tm_exchange(packed)
    ahead_scratch = [
        pltpu.VMEM((rows + 2, (cols + 2) * total, channels), bf16),
        pltpu.VMEM((9 * wide // lanes, chunk_rows(rows, total) * (cols + 2) * total, lanes), f32),
    ]
    flops = 2 * 27 * width * channels * total * count
    sums = call(
        functools.partial(both_kernel, peers, frames, rows, channels),
        [struct((frames, count, channels + wide), bf16)] * peers,
        [
            pltpu.VMEM(((channels + wide) // lanes, plane * total, lanes), f32),
            pltpu.VMEM((rows + 2, cols * total, 3 * wide), bf16),
            *ahead_scratch,
            pltpu.VMEM((channels // lanes, count * total, lanes), f32),
            pltpu.VMEM((wide // lanes, count * total, lanes), f32),
        ],
        2 * flops,
        spare=8,
        name="both",
    )(*got, first_kernel, second_kernel)
    got = tm_exchange(sums)
    hidden_grad = call(
        functools.partial(middle_kernel, peers, width),
        [struct(features.shape, bf16)],
        [pltpu.VMEM((frames, count, channels), f32)],
        name="middle",
    )(*got, gain_two, first_bias[None])[0]
    hidden_plane = with_halo(with_halo(hidden_grad, "col", 2), "row", 1)
    got = tm_exchange([hidden_plane.reshape(frames, plane, channels)] * peers)
    backs = call(
        functools.partial(back_kernel, peers, frames, rows),
        [struct((frames, count, wide), bf16)] * peers,
        [
            pltpu.VMEM((channels // lanes, plane * total, lanes), f32),
            *ahead_scratch,
            pltpu.VMEM((wide // lanes, count * total, lanes), f32),
        ],
        flops,
        spare=8,
        name="back",
    )(*got, first_kernel)
    got = tm_exchange(backs)
    by_col = (0, 2, 1, 3)
    held = features.transpose(by_col), reward_grad.transpose(by_col)
    result = call(
        functools.partial(final_kernel, peers, width),
        [struct(held[0].shape, bf16)],
        [pltpu.VMEM((frames, 3, count, channels), f32)],
        name="final",
    )(*got, *held, gain_one)[0]
    return result.transpose(by_col)


def solution(mesh):
    in_specs = (
        P("tm", "row", "col", None),
        P("tm", "row", "col", None),
        P(None, None, None, "tm", None),
        P(None, None, None, "tm", None),
        P(),
        P(),
        P(),
    )
    out_specs = P("tm", "row", "col", None)
    return jax.shard_map(
        on_device, mesh=mesh, in_specs=in_specs, out_specs=out_specs, check_vma=False
    )
```

```python
import functools
import math

import jax
import jax.numpy as jnp
from jax import lax
from jax.experimental import pallas as pl
from jax.experimental.pallas import tpu as pltpu
from jax.sharding import PartitionSpec as P

epsilon = 1e-06
f32 = jnp.float32
bf16 = jnp.bfloat16
lanes = 128


def is_power(count):
    return count & (count - 1) == 0


def sent_to(index, step, count):
    return index ^ step if is_power(count) else lax.rem(index + step, count)


def got_from(index, step, count):
    return index ^ step if is_power(count) else lax.rem(index + count - step, count)


def tm_exchange(blocks):
    count = len(blocks)
    got = [blocks[0]]
    for step in range(1, count):
        pairs = [
            (i, i ^ step if is_power(count) else (i + step) % count) for i in range(count)
        ]
        got.append(lax.ppermute(blocks[step], "tm", pairs))
    return got


def is_even(axis):
    return lax.rem(lax.axis_index(axis), 2) == 0


def halo_swaps(low_edge, high_edge, axis):
    count = lax.axis_size(axis)
    even = is_even(axis)
    got = []
    for start, value in ((0, (high_edge, low_edge)), (1, (low_edge, high_edge))):
        pairs = [(i, i + 1) for i in range(start, count - 1, 2)]
        if pairs:
            pairs = pairs + [(b, a) for a, b in pairs]
            got.append(lax.ppermute(jnp.where(even, *value), axis, pairs))
        else:
            got.append(None)
    return got


def low_and_high(axis, first, second):
    even = is_even(axis)
    if first is None:
        return None, None
    nothing = jnp.zeros_like(first)
    second = nothing if second is None else second
    return jnp.where(even, second, first), jnp.where(even, first, second)


def halo_edges(blocks, rows):
    count = blocks[0].shape[1]
    left = jnp.stack([block[:, :rows] for block in blocks])
    right = jnp.stack([block[:, count - rows :] for block in blocks])
    sides = halo_swaps(left, right, "col")
    low_side, high_side = low_and_high("col", *sides)
    if low_side is None:
        low_side = high_side = jnp.zeros_like(left)

    def strip(row):
        own = jnp.stack([block[:, row::rows] for block in blocks])
        return jnp.concatenate(
            [low_side[:, :, row : row + 1], own, high_side[:, :, row : row + 1]], axis=2
        )

    ends = halo_swaps(strip(0), strip(rows - 1), "row")
    return [[got for got in part if got is not None] for part in (sides, ends)]


def rms_parts(values, gain):
    inv_rms = lax.rsqrt(jnp.mean(values * values, axis=-1, keepdims=True) + epsilon)
    normed = values * inv_rms
    return inv_rms, normed, normed * gain


def silu_slope(values):
    sigmoid_val = jax.nn.sigmoid(values)
    return sigmoid_val * (1.0 + values * (1.0 - sigmoid_val))


def rms_back(cotangent, inv_rms, normed, gain):
    scaled_grad = cotangent * gain
    return inv_rms * (scaled_grad - normed * jnp.mean(normed * scaled_grad, axis=-1, keepdims=True))


def slot_matrix(slot, width, channels, wide):
    row = lax.broadcasted_iota(jnp.int32, (channels, wide), 0)
    col = lax.broadcasted_iota(jnp.int32, (channels, wide), 1)
    hit = (row == col + slot * width) & (col < width)
    return jnp.where(hit, 1.0, 0.0).astype(bf16)


def spread_matrix(slot, width, channels, wide):
    row = lax.broadcasted_iota(jnp.int32, (wide, channels), 0)
    col = lax.broadcasted_iota(jnp.int32, (wide, channels), 1)
    hit = (col == row + slot * width) & (row < width)
    return jnp.where(hit, 1.0, 0.0).astype(bf16)


def pack_kernel(peers, width, both_ref, gain_ref, *refs):
    out_refs, flat_ref = refs[:-1], refs[-1]
    me = lax.axis_index("tm")
    feat_ref, reward_ref = both_ref.at[0], both_ref.at[1]
    frames, channels = feat_ref.shape[0], feat_ref.shape[3]
    wide = out_refs[0].shape[2] - channels
    for frame in range(frames):
        act = rms_parts(join_cells(flat_ref.at[frame, 0], feat_ref, frame), gain_ref[...])[2]
        silu = (act * jax.nn.sigmoid(act)).astype(bf16)
        reward = join_cells(flat_ref.at[frame, 1], reward_ref, frame).astype(bf16)
        for step in range(peers):
            slot = sent_to(me, step, peers)
            piece = jnp.dot(
                silu, slot_matrix(slot, width, channels, wide), preferred_element_type=f32
            )
            out_refs[step][frame, :, :channels] = reward
            out_refs[step][frame, :, channels:] = piece.astype(bf16)


class Cells:
    def __init__(self, rows, cols):
        self.rows, self.cols = rows, cols
        self.left = rows * cols
        self.right = self.left + rows
        self.low = self.right + rows
        self.high = self.low + cols + 2

    def at(self, row, col):
        if row == 0:
            return self.low + col
        if row == self.rows + 1:
            return self.high + col
        if col == 0:
            return self.left + row - 1
        if col == self.cols + 1:
            return self.right + row - 1
        return (col - 1) * self.rows + row - 1


def lay_frames(peers, frames, cells, block_refs, side_refs, end_refs, cells_ref):
    me = lax.axis_index("tm")
    total = peers * frames
    tiles = cells_ref.shape[0]

    def lay(start, frame, values):
        for tile in range(tiles):
            piece = values[:, tile * lanes : (tile + 1) * lanes]
            place = pl.ds(start * total + frame, piece.shape[0], stride=total)
            cells_ref[tile, place, :] = piece.astype(f32)

    for step in range(peers):
        source = got_from(me, step, peers)
        for frame in range(frames):
            at = source * frames + frame
            lay(0, at, block_refs[step][frame])
            for axis, got_refs, low, high, count in (
                ("col", side_refs, cells.left, cells.right, cells.rows),
                ("row", end_refs, cells.low, cells.high, cells.cols + 2),
            ):
                got = [ref[step, frame].astype(f32) for ref in got_refs] + [None, None]
                values = low_and_high(axis, got[0], got[1])
                for start, value in zip((low, high), values):
                    if value is None:
                        value = jnp.zeros((count, tiles * lanes), f32)
                    lay(start, at, value)


def plane_row(cells, cells_ref, tile, row, first, count, total):
    return jnp.concatenate(
        [
            cells_ref[tile, pl.ds(cells.at(row, first + col) * total, total), :]
            for col in range(count)
        ],
        axis=0,
    )


def shifted(values, ahead):
    total = values.shape[1]
    if ahead == 0:
        return values
    frame = lax.broadcasted_iota(jnp.int32, values.shape, 1)
    moved = pltpu.roll(values, (-ahead) % total, 1)
    keep = frame < total - ahead if ahead > 0 else frame >= -ahead
    return jnp.where(keep, moved, 0.0)


def chunk_rows(rows, total):
    return max(r for r in range(1, rows + 1) if rows % r == 0 and (r == 1 or r * total <= 32))


def stacked_weights(kernel_ref, wide, order):
    width, channels = kernel_ref.shape[3:]
    pad = jnp.zeros((wide - width, channels), bf16)

    def block(a, b, c):
        value = kernel_ref[a, b, c]
        return jnp.concatenate([value, pad], axis=0) if wide > width else value

    return jnp.concatenate(
        [jnp.concatenate([block(*tap) for tap in column], axis=0) for column in order], axis=1
    )


def conv_ahead(cells, cells_ref, first, kernel_ref, plane_ref, parts_ref, sum_ref, total):
    rows, cols, channels = cells.rows, cells.cols, plane_ref.shape[2]
    wide = sum_ref.shape[0] * lanes
    wide_tiles = wide // lanes
    for row in range(rows + 2):
        for tile in range(channels // lanes):
            plane_ref[row, :, tile * lanes : (tile + 1) * lanes] = plane_row(
                cells, cells_ref, first + tile, row, 0, cols + 2, total
            ).astype(bf16)

    weights = stacked_weights(
        kernel_ref,
        wide,
        [[(2 - s, 2 - b, 2 - c) for s in range(3) for c in range(3)] for b in range(3)],
    )
    step = chunk_rows(rows, total)

    def chunk(start):
        left = jnp.concatenate(
            [plane_ref[pl.ds(start + b, step)].reshape(-1, channels) for b in range(3)], axis=1
        )
        parts = lax.dot_general(left, weights, (((1,), (1,)), ((), ())), preferred_element_type=f32)
        for tile in range(parts_ref.shape[0]):
            parts_ref[tile] = parts[:, tile * lanes : (tile + 1) * lanes]
        for row in range(step):
            for tile in range(wide_tiles):
                summed = None
                for s in range(3):
                    part = None
                    for c in range(3):
                        at = (row * (cols + 2) + c) * total
                        piece = parts_ref[(s * 3 + c) * wide_tiles + tile, at : at + cols * total, :]
                        part = piece if part is None else part + piece
                    part = shifted(part.reshape(cols, total, lanes), s)
                    summed = part if summed is None else summed + part
                for col in range(cols):
                    place = pl.ds((col * rows + start + row) * total, total)
                    sum_ref[tile, place, :] = summed[col]

    run_chunks(rows, step, chunk)


def run_chunks(rows, step, chunk):
    if step == rows:
        chunk(0)
    else:
        pl.loop(0, rows, step=step)(chunk)


def conv_behind(cells, cells_ref, first, kernel_ref, taps_ref, sum_ref, total):
    rows, cols = cells.rows, cells.cols
    channels = sum_ref.shape[0] * lanes
    wide_tiles = taps_ref.shape[2] // (3 * lanes)
    for row in range(rows + 2):
        for tile in range(wide_tiles):
            for c in range(3):
                at = (c * wide_tiles + tile) * lanes
                taps_ref[row, :, at : at + lanes] = plane_row(
                    cells, cells_ref, first + tile, row, c, cols, total
                ).astype(bf16)

    weights = stacked_weights(
        kernel_ref,
        wide_tiles * lanes,
        [[(a, b, c) for b in range(3) for c in range(3)] for a in range(3)],
    )
    step = chunk_rows(rows, total)

    def chunk(start):
        left = jnp.concatenate(
            [
                taps_ref[pl.ds(start + b, step)].reshape(-1, taps_ref.shape[2])
                for b in range(3)
            ],
            axis=1,
        )
        parts = jnp.dot(left, weights, preferred_element_type=f32)
        for tile in range(channels // lanes):
            summed = None
            for a in range(3):
                at = a * channels + tile * lanes
                part = parts[:, at : at + lanes].reshape(step * cols, total, lanes)
                part = shifted(part, a - 2)
                summed = part if summed is None else summed + part
            for row in range(step):
                for col in range(cols):
                    place = pl.ds((col * rows + start + row) * total, total)
                    sum_ref[tile, place, :] = summed[row * cols + col]

    run_chunks(rows, step, chunk)


def hand_out(peers, frames, total, sum_ref, out_refs, start):
    me = lax.axis_index("tm")
    for step in range(peers):
        target = sent_to(me, step, peers)
        for frame in range(frames):
            place = pl.ds(target * frames + frame, out_refs[step].shape[1], stride=total)
            for tile in range(sum_ref.shape[0]):
                at = start + tile * lanes
                out_refs[step][frame, :, at : at + lanes] = sum_ref[tile, place, :].astype(bf16)


def inner_kernel(peers, frames, cells, sides, behind, *refs):
    blocks, side_refs, refs = refs[:peers], refs[peers : peers + sides], refs[peers + sides :]
    total = peers * frames
    if behind:
        kernel_one, kernel_two, sum_one, sum_two, cells_ref, plane, parts, taps = refs
    else:
        kernel_two, sum_two, cells_ref, plane, parts = refs
    lay_frames(peers, frames, cells, blocks, side_refs, [], cells_ref)
    if behind:
        tiles = plane.shape[2] // lanes
        conv_behind(cells, cells_ref, tiles, kernel_one, taps, sum_one, total)
    conv_ahead(cells, cells_ref, 0, kernel_two, plane, parts, sum_two, total)


def outer_kernel(peers, frames, cells, ends, behind, *refs):
    end_refs, refs = refs[:ends], refs[ends:]
    count = 2 if behind else 1
    kernels, sums, outs = refs[:count], refs[count : 2 * count], refs[2 * count : 2 * count + peers]
    cells_ref, *kept = refs[2 * count + peers :]
    total = peers * frames
    me = lax.axis_index("tm")
    span = cells.cols + 2
    for step in range(peers):
        source = got_from(me, step, peers)
        for frame in range(frames):
            got = [ref[step, frame].astype(f32) for ref in end_refs] + [None, None]
            values = low_and_high("row", got[0], got[1])
            for place, value in enumerate(values):
                for tile in range(cells_ref.shape[0]):
                    at = place * span * total + source * frames + frame
                    cells_ref[tile, pl.ds(at, span, stride=total), :] = value[
                        :, tile * lanes : (tile + 1) * lanes
                    ]
    for kernel_ref, sum_ref, out_ref in zip(kernels, sums, kept):
        for tile in range(sum_ref.shape[0]):
            out_ref[tile] = sum_ref[tile]
    for place, row in ((0, 0), (1, cells.rows - 1)):
        if behind:
            outer_behind(cells, cells_ref, place, row, kernels[0], kept[0], total)
        outer_ahead(cells, cells_ref, place, row, kernels[-1], kept[-1], total)
    start = 0
    for sum_ref in kept:
        hand_out(peers, frames, total, sum_ref, outs, start)
        start += sum_ref.shape[0] * lanes


def add_row(cells, sum_ref, tile, row, values, total):
    for col in range(cells.cols):
        place = pl.ds((col * cells.rows + row) * total, total)
        sum_ref[tile, place, :] = sum_ref[tile, place, :] + values[col]


def end_row(cells, cells_ref, place, first, count, start, cols, total):
    base = (place * (cells.cols + 2) + start) * total
    return jnp.concatenate(
        [cells_ref[first + tile, base : base + cols * total, :] for tile in range(count)], axis=1
    ).astype(bf16)


def outer_behind(cells, cells_ref, place, row, kernel_ref, sum_ref, total):
    cols, channels = cells.cols, sum_ref.shape[0] * lanes
    tiles = channels // lanes
    wide_tiles = cells_ref.shape[0] - tiles
    b = 2 * place
    weights = stacked_weights(
        kernel_ref, wide_tiles * lanes, [[(a, b, c) for c in range(3)] for a in range(3)]
    )
    left = jnp.concatenate(
        [end_row(cells, cells_ref, place, tiles, wide_tiles, c, cols, total) for c in range(3)],
        axis=1,
    )
    parts = jnp.dot(left, weights, preferred_element_type=f32)
    for tile in range(tiles):
        summed = None
        for a in range(3):
            at = a * channels + tile * lanes
            part = shifted(parts[:, at : at + lanes].reshape(cols, total, lanes), a - 2)
            summed = part if summed is None else summed + part
        add_row(cells, sum_ref, tile, row, summed, total)


def outer_ahead(cells, cells_ref, place, row, kernel_ref, sum_ref, total):
    cols, channels = cells.cols, kernel_ref.shape[4]
    wide = sum_ref.shape[0] * lanes
    b = 2 * place
    weights = stacked_weights(
        kernel_ref, wide, [[(2 - s, 2 - b, 2 - c) for s in range(3) for c in range(3)]]
    )
    left = end_row(cells, cells_ref, place, 0, channels // lanes, 0, cols + 2, total)
    parts = lax.dot_general(left, weights, (((1,), (1,)), ((), ())), preferred_element_type=f32)
    for tile in range(wide // lanes):
        summed = None
        for s in range(3):
            part = None
            for c in range(3):
                at = (s * 3 + c) * wide + tile * lanes
                piece = parts[c * total : (c + cols) * total, at : at + lanes]
                part = piece if part is None else part + piece
            part = shifted(part.reshape(cols, total, lanes), s)
            summed = part if summed is None else summed + part
        add_row(cells, sum_ref, tile, row, summed, total)


def gathered(peers, frame, block_refs, start, width, channels):
    me = lax.axis_index("tm")
    wide = block_refs[0].shape[2] - start
    summed = None
    for step in range(peers):
        spread = spread_matrix(got_from(me, step, peers), width, channels, wide)
        part = jnp.dot(
            block_refs[step][frame, :, start:], spread, preferred_element_type=f32
        )
        summed = part if summed is None else summed + part
    return summed


def join_cells(flat_ref, in_ref, frame):
    rows = in_ref.shape[2]
    for col in range(in_ref.shape[1]):
        flat_ref[col * rows : (col + 1) * rows, :] = in_ref[frame, col].astype(f32)
    return flat_ref[...]


def split_cells(flat_ref, values, out_ref, frame):
    flat_ref[...] = values
    rows = out_ref.shape[2]
    for col in range(out_ref.shape[1]):
        out_ref[frame, col] = flat_ref[col * rows : (col + 1) * rows, :].astype(bf16)


def middle_kernel(peers, width, *refs):
    blocks = refs[:peers]
    gain_ref, bias_ref, out_ref = refs[peers:]
    frames, _, channels = out_ref.shape
    for frame in range(frames):
        hidden = blocks[0][frame, :, :channels].astype(f32)
        for step in range(1, peers):
            hidden = hidden + blocks[step][frame, :, :channels].astype(f32)
        hidden = hidden + bias_ref[...]
        back = gathered(peers, frame, blocks, channels, width, channels)
        inv, normed, act = rms_parts(hidden, gain_ref[...])
        out_ref[frame] = rms_back(back * silu_slope(act), inv, normed, gain_ref[...]).astype(bf16)


def final_kernel(peers, width, *refs):
    blocks = refs[:peers]
    feat_ref, reward_ref, gain_ref, out_ref, flat_ref = refs[peers:]
    frames, channels = out_ref.shape[0], out_ref.shape[3]
    for frame in range(frames):
        back = gathered(peers, frame, blocks, 0, width, channels)
        values = join_cells(flat_ref.at[frame, 0], feat_ref, frame)
        reward = join_cells(flat_ref.at[frame, 1], reward_ref, frame)
        inv, normed, act = rms_parts(values, gain_ref[...])
        result = rms_back(back * silu_slope(act), inv, normed, gain_ref[...])
        split_cells(flat_ref.at[frame, 2], result + reward, out_ref, frame)


def size_of(structs):
    return sum(math.prod(s.shape) * s.dtype.itemsize for s in structs)


def call(kernel, outs, scratch=(), flops=0, spare=2, covered=0, name=None):
    def run(*operands):
        held = size_of(outs) + size_of(operands)
        grant = 2 * held + size_of(scratch) + spare * 2**20
        return pl.pallas_call(
            kernel,
            out_shape=outs,
            scratch_shapes=list(scratch),
            cost_estimate=pl.CostEstimate(
                flops=flops + covered, bytes_accessed=held, transcendentals=0
            ),
            compiler_params=pltpu.CompilerParams(vmem_limit_bytes=min(grant, 60 * 2**20)),
            name=name,
        )(*operands)

    return run


def on_device(
    features, reward_grad, first_kernel, second_kernel, first_gain, second_gain, first_bias
):
    peers = lax.axis_size("tm")
    frames, rows, cols, channels = features.shape
    width = first_kernel.shape[3]
    wide = -(-width // lanes) * lanes
    total = peers * frames
    plane = (rows + 2) * (cols + 2)
    count = rows * cols
    struct = jax.ShapeDtypeStruct

    cells = Cells(rows, cols)
    by_col = (0, 2, 1, 3)
    held = features.transpose(by_col), reward_grad.transpose(by_col)
    ahead_scratch = [
        pltpu.VMEM((rows + 2, (cols + 2) * total, channels), bf16),
        pltpu.VMEM((9 * wide // lanes, chunk_rows(rows, total) * (cols + 2) * total, lanes), f32),
    ]
    flops = 2 * 27 * width * channels * total * count
    sum_shapes = [
        (channels // lanes, count * total, lanes),
        (wide // lanes, count * total, lanes),
    ]

    def convolved(blocks, kernels):
        behind = len(kernels) == 2
        shapes = sum_shapes[-len(kernels) :]
        tiles = blocks[0].shape[2] // lanes
        sides, ends = halo_edges(blocks, rows)
        taps = [pltpu.VMEM((rows + 2, cols * total, 3 * wide), bf16)] if behind else []
        sums = call(
            functools.partial(inner_kernel, peers, frames, cells, len(sides), behind),
            [struct(shape, f32) for shape in shapes],
            [pltpu.VMEM((tiles, plane * total, lanes), f32), *ahead_scratch, *taps],
            flops * len(kernels),
            spare=8,
            name="inner",
        )(*blocks, *sides, *kernels)
        return call(
            functools.partial(outer_kernel, peers, frames, cells, len(ends), behind),
            [struct((frames, count, sum(s[0] for s in shapes) * lanes), bf16)] * peers,
            [
                pltpu.VMEM((tiles, 2 * (cols + 2) * total, lanes), f32),
                *[pltpu.VMEM(shape, f32) for shape in shapes],
            ],
            flops * len(kernels) // 6,
            spare=8,
            name="outer",
        )(*ends, *kernels, *sums)

    packed = call(
        functools.partial(pack_kernel, peers, width),
        [struct((frames, count, channels + wide), bf16)] * peers,
        [pltpu.VMEM((frames, 2, count, channels), f32)],
        covered=4 * 10**9,
        name="pack",
    )(jnp.stack(held), first_gain)
    sums = convolved(tm_exchange(packed), [first_kernel, second_kernel])
    got = tm_exchange(sums)
    hidden_grad = call(
        functools.partial(middle_kernel, peers, width),
        [struct((frames, count, channels), bf16)],
        name="middle",
    )(*got, second_gain, first_bias)[0]
    backs = convolved(tm_exchange([hidden_grad] * peers), [first_kernel])
    got = tm_exchange(backs)
    result = call(
        functools.partial(final_kernel, peers, width),
        [struct(held[0].shape, bf16)],
        [pltpu.VMEM((frames, 3, count, channels), f32)],
        name="final",
    )(*got, *held, first_gain)[0]
    return result.transpose(by_col)


def solution(mesh):
    in_specs = (
        P("tm", "row", "col", None),
        P("tm", "row", "col", None),
        P(None, None, None, "tm", None),
        P(None, None, None, "tm", None),
        P(),
        P(),
        P(),
    )
    out_specs = P("tm", "row", "col", None)
    return jax.shard_map(
        on_device, mesh=mesh, in_specs=in_specs, out_specs=out_specs, check_vma=False
    )
```

```python
import functools
import math

import jax
import jax.numpy as jnp
from jax import lax
from jax.experimental import pallas as pl
from jax.experimental.pallas import tpu as pltpu
from jax.sharding import PartitionSpec as P

epsilon = 1e-06
f32 = jnp.float32
bf16 = jnp.bfloat16
lanes = 128


def is_power(count):
    return count & (count - 1) == 0


def sent_to(index, step, count):
    return index ^ step if is_power(count) else lax.rem(index + step, count)


def got_from(index, step, count):
    return index ^ step if is_power(count) else lax.rem(index + count - step, count)


def tm_exchange(blocks):
    count = len(blocks)
    got = [blocks[0]]
    for step in range(1, count):
        pairs = [
            (i, i ^ step if is_power(count) else (i + step) % count) for i in range(count)
        ]
        got.append(lax.ppermute(blocks[step], "tm", pairs))
    return got


def is_even(axis):
    return lax.rem(lax.axis_index(axis), 2) == 0


def halo_swaps(low_edge, high_edge, axis):
    count = lax.axis_size(axis)
    even = is_even(axis)
    got = []
    for start, value in ((0, (high_edge, low_edge)), (1, (low_edge, high_edge))):
        pairs = [(i, i + 1) for i in range(start, count - 1, 2)]
        if pairs:
            pairs = pairs + [(b, a) for a, b in pairs]
            got.append(lax.ppermute(jnp.where(even, *value), axis, pairs))
        else:
            got.append(None)
    return got


def low_and_high(axis, first, second):
    even = is_even(axis)
    if first is None:
        return None, None
    nothing = jnp.zeros_like(first)
    second = nothing if second is None else second
    return jnp.where(even, second, first), jnp.where(even, first, second)


def halo_edges(blocks, rows):
    count = blocks[0].shape[1]
    left = jnp.stack([block[:, :rows] for block in blocks])
    right = jnp.stack([block[:, count - rows :] for block in blocks])
    sides = halo_swaps(left, right, "col")
    low_side, high_side = low_and_high("col", *sides)
    if low_side is None:
        low_side = high_side = jnp.zeros_like(left)

    def strip(row):
        own = jnp.stack([block[:, row::rows] for block in blocks])
        return jnp.concatenate(
            [low_side[:, :, row : row + 1], own, high_side[:, :, row : row + 1]], axis=2
        )

    ends = halo_swaps(strip(0), strip(rows - 1), "row")
    return [[got for got in part if got is not None] for part in (sides, ends)]


def rms_parts(values, gain):
    inv_rms = lax.rsqrt(jnp.mean(values * values, axis=-1, keepdims=True) + epsilon)
    normed = values * inv_rms
    return inv_rms, normed, normed * gain


def silu_slope(values):
    sigmoid_val = jax.nn.sigmoid(values)
    return sigmoid_val * (1.0 + values * (1.0 - sigmoid_val))


def rms_back(cotangent, inv_rms, normed, gain):
    scaled_grad = cotangent * gain
    return inv_rms * (scaled_grad - normed * jnp.mean(normed * scaled_grad, axis=-1, keepdims=True))


def slot_matrix(slot, width, channels, wide):
    row = lax.broadcasted_iota(jnp.int32, (channels, wide), 0)
    col = lax.broadcasted_iota(jnp.int32, (channels, wide), 1)
    hit = (row == col + slot * width) & (col < width)
    return jnp.where(hit, 1.0, 0.0).astype(bf16)


def spread_matrix(slot, width, channels, wide):
    row = lax.broadcasted_iota(jnp.int32, (wide, channels), 0)
    col = lax.broadcasted_iota(jnp.int32, (wide, channels), 1)
    hit = (col == row + slot * width) & (row < width)
    return jnp.where(hit, 1.0, 0.0).astype(bf16)


def pack_kernel(peers, width, both_ref, gain_ref, *refs):
    out_refs, flat_ref = refs[:-1], refs[-1]
    me = lax.axis_index("tm")
    feat_ref, reward_ref = both_ref.at[0], both_ref.at[1]
    frames, channels = feat_ref.shape[0], feat_ref.shape[3]
    wide = out_refs[0].shape[2] - channels
    for frame in range(frames):
        act = rms_parts(join_cells(flat_ref.at[frame, 0], feat_ref, frame), gain_ref[...])[2]
        silu = (act * jax.nn.sigmoid(act)).astype(bf16)
        reward = join_cells(flat_ref.at[frame, 1], reward_ref, frame).astype(bf16)
        for step in range(peers):
            slot = sent_to(me, step, peers)
            piece = jnp.dot(
                silu, slot_matrix(slot, width, channels, wide), preferred_element_type=f32
            )
            out_refs[step][frame, :, :channels] = reward
            out_refs[step][frame, :, channels:] = piece.astype(bf16)


class Cells:
    def __init__(self, rows, cols):
        self.rows, self.cols = rows, cols
        self.left = rows * cols
        self.right = self.left + rows
        self.low = self.right + rows
        self.high = self.low + cols + 2

    def at(self, row, col):
        if row == 0:
            return self.low + col
        if row == self.rows + 1:
            return self.high + col
        if col == 0:
            return self.left + row - 1
        if col == self.cols + 1:
            return self.right + row - 1
        return (col - 1) * self.rows + row - 1


def lay_frames(peers, frames, cells, block_refs, side_refs, end_refs, cells_ref):
    me = lax.axis_index("tm")
    total = peers * frames
    tiles = cells_ref.shape[0]

    def lay(start, frame, values):
        for tile in range(tiles):
            piece = values[:, tile * lanes : (tile + 1) * lanes]
            place = pl.ds(start * total + frame, piece.shape[0], stride=total)
            cells_ref[tile, place, :] = piece.astype(f32)

    for step in range(peers):
        source = got_from(me, step, peers)
        for frame in range(frames):
            at = source * frames + frame
            lay(0, at, block_refs[step][frame])
            for axis, got_refs, low, high, count in (
                ("col", side_refs, cells.left, cells.right, cells.rows),
                ("row", end_refs, cells.low, cells.high, cells.cols + 2),
            ):
                got = [ref[step, frame].astype(f32) for ref in got_refs] + [None, None]
                values = low_and_high(axis, got[0], got[1])
                for start, value in zip((low, high), values):
                    if value is None:
                        value = jnp.zeros((count, tiles * lanes), f32)
                    lay(start, at, value)


def plane_row(cells, cells_ref, tile, row, first, count, total):
    return jnp.concatenate(
        [
            cells_ref[tile, pl.ds(cells.at(row, first + col) * total, total), :]
            for col in range(count)
        ],
        axis=0,
    )


def shifted(values, ahead):
    total = values.shape[1]
    if ahead == 0:
        return values
    frame = lax.broadcasted_iota(jnp.int32, values.shape, 1)
    moved = pltpu.roll(values, (-ahead) % total, 1)
    keep = frame < total - ahead if ahead > 0 else frame >= -ahead
    return jnp.where(keep, moved, 0.0)


def chunk_rows(rows, total):
    return max(r for r in range(1, rows + 1) if rows % r == 0 and (r == 1 or r * total <= 32))


def stacked_weights(kernel_ref, wide, order):
    width, channels = kernel_ref.shape[3:]
    pad = jnp.zeros((wide - width, channels), bf16)

    def block(a, b, c):
        value = kernel_ref[a, b, c]
        return jnp.concatenate([value, pad], axis=0) if wide > width else value

    return jnp.concatenate(
        [jnp.concatenate([block(*tap) for tap in column], axis=0) for column in order], axis=1
    )


def conv_ahead(cells, cells_ref, first, kernel_ref, plane_ref, parts_ref, sum_ref, total):
    rows, cols, channels = cells.rows, cells.cols, plane_ref.shape[2]
    wide = sum_ref.shape[0] * lanes
    wide_tiles = wide // lanes
    for row in range(rows + 2):
        for tile in range(channels // lanes):
            plane_ref[row, :, tile * lanes : (tile + 1) * lanes] = plane_row(
                cells, cells_ref, first + tile, row, 0, cols + 2, total
            ).astype(bf16)

    weights = stacked_weights(
        kernel_ref,
        wide,
        [[(2 - s, 2 - b, 2 - c) for s in range(3) for c in range(3)] for b in range(3)],
    )
    step = chunk_rows(rows, total)

    def chunk(start):
        left = jnp.concatenate(
            [plane_ref[pl.ds(start + b, step)].reshape(-1, channels) for b in range(3)], axis=1
        )
        parts = lax.dot_general(left, weights, (((1,), (1,)), ((), ())), preferred_element_type=f32)
        for tile in range(parts_ref.shape[0]):
            parts_ref[tile] = parts[:, tile * lanes : (tile + 1) * lanes]
        for row in range(step):
            for tile in range(wide_tiles):
                summed = None
                for s in range(3):
                    part = None
                    for c in range(3):
                        at = (row * (cols + 2) + c) * total
                        piece = parts_ref[(s * 3 + c) * wide_tiles + tile, at : at + cols * total, :]
                        part = piece if part is None else part + piece
                    part = shifted(part.reshape(cols, total, lanes), s)
                    summed = part if summed is None else summed + part
                for col in range(cols):
                    place = pl.ds((col * rows + start + row) * total, total)
                    sum_ref[tile, place, :] = summed[col]

    run_chunks(rows, step, chunk)


def run_chunks(rows, step, chunk):
    if step == rows:
        chunk(0)
    else:
        pl.loop(0, rows, step=step)(chunk)


def conv_behind(cells, cells_ref, first, kernel_ref, taps_ref, sum_ref, total):
    rows, cols = cells.rows, cells.cols
    channels = sum_ref.shape[0] * lanes
    wide_tiles = taps_ref.shape[2] // (3 * lanes)
    for row in range(rows + 2):
        for tile in range(wide_tiles):
            for c in range(3):
                at = (c * wide_tiles + tile) * lanes
                taps_ref[row, :, at : at + lanes] = plane_row(
                    cells, cells_ref, first + tile, row, c, cols, total
                ).astype(bf16)

    weights = stacked_weights(
        kernel_ref,
        wide_tiles * lanes,
        [[(a, b, c) for b in range(3) for c in range(3)] for a in range(3)],
    )
    step = chunk_rows(rows, total)

    def chunk(start):
        left = jnp.concatenate(
            [
                taps_ref[pl.ds(start + b, step)].reshape(-1, taps_ref.shape[2])
                for b in range(3)
            ],
            axis=1,
        )
        parts = jnp.dot(left, weights, preferred_element_type=f32)
        for tile in range(channels // lanes):
            summed = None
            for a in range(3):
                at = a * channels + tile * lanes
                part = parts[:, at : at + lanes].reshape(step * cols, total, lanes)
                part = shifted(part, a - 2)
                summed = part if summed is None else summed + part
            for row in range(step):
                for col in range(cols):
                    place = pl.ds((col * rows + start + row) * total, total)
                    sum_ref[tile, place, :] = summed[row * cols + col]

    run_chunks(rows, step, chunk)


def hand_out(peers, frames, total, sum_ref, out_refs, start):
    me = lax.axis_index("tm")
    for step in range(peers):
        target = sent_to(me, step, peers)
        for frame in range(frames):
            place = pl.ds(target * frames + frame, out_refs[step].shape[1], stride=total)
            for tile in range(sum_ref.shape[0]):
                at = start + tile * lanes
                out_refs[step][frame, :, at : at + lanes] = sum_ref[tile, place, :].astype(bf16)


def inner_kernel(peers, frames, cells, sides, behind, *refs):
    blocks, side_refs, refs = refs[:peers], refs[peers : peers + sides], refs[peers + sides :]
    total = peers * frames
    if behind:
        kernel_one, kernel_two, sum_one, sum_two, cells_ref, plane, parts, taps = refs
    else:
        kernel_two, sum_two, cells_ref, plane, parts = refs
    lay_frames(peers, frames, cells, blocks, side_refs, [], cells_ref)
    if behind:
        tiles = plane.shape[2] // lanes
        conv_behind(cells, cells_ref, tiles, kernel_one, taps, sum_one, total)
    conv_ahead(cells, cells_ref, 0, kernel_two, plane, parts, sum_two, total)


def outer_kernel(peers, frames, cells, ends, behind, *refs):
    end_refs, refs = refs[:ends], refs[ends:]
    count = 2 if behind else 1
    kernels, sums, outs = refs[:count], refs[count : 2 * count], refs[2 * count : 2 * count + peers]
    cells_ref, *kept = refs[2 * count + peers :]
    total = peers * frames
    me = lax.axis_index("tm")
    span = cells.cols + 2
    for step in range(peers):
        source = got_from(me, step, peers)
        for frame in range(frames):
            got = [ref[step, frame].astype(f32) for ref in end_refs] + [None, None]
            values = low_and_high("row", got[0], got[1])
            for place, value in enumerate(values):
                for tile in range(cells_ref.shape[0]):
                    at = place * span * total + source * frames + frame
                    cells_ref[tile, pl.ds(at, span, stride=total), :] = value[
                        :, tile * lanes : (tile + 1) * lanes
                    ]
    for kernel_ref, sum_ref, out_ref in zip(kernels, sums, kept):
        for tile in range(sum_ref.shape[0]):
            out_ref[tile] = sum_ref[tile]
    for place, row in ((0, 0), (1, cells.rows - 1)):
        if behind:
            outer_behind(cells, cells_ref, place, row, kernels[0], kept[0], total)
        outer_ahead(cells, cells_ref, place, row, kernels[-1], kept[-1], total)
    start = 0
    for sum_ref in kept:
        hand_out(peers, frames, total, sum_ref, outs, start)
        start += sum_ref.shape[0] * lanes


def add_row(cells, sum_ref, tile, row, values, total):
    for col in range(cells.cols):
        place = pl.ds((col * cells.rows + row) * total, total)
        sum_ref[tile, place, :] = sum_ref[tile, place, :] + values[col]


def end_row(cells, cells_ref, place, first, count, start, cols, total):
    base = (place * (cells.cols + 2) + start) * total
    return jnp.concatenate(
        [cells_ref[first + tile, base : base + cols * total, :] for tile in range(count)], axis=1
    ).astype(bf16)


def outer_behind(cells, cells_ref, place, row, kernel_ref, sum_ref, total):
    cols, channels = cells.cols, sum_ref.shape[0] * lanes
    tiles = channels // lanes
    wide_tiles = cells_ref.shape[0] - tiles
    b = 2 * place
    weights = stacked_weights(
        kernel_ref, wide_tiles * lanes, [[(a, b, c) for c in range(3)] for a in range(3)]
    )
    left = jnp.concatenate(
        [end_row(cells, cells_ref, place, tiles, wide_tiles, c, cols, total) for c in range(3)],
        axis=1,
    )
    parts = jnp.dot(left, weights, preferred_element_type=f32)
    for tile in range(tiles):
        summed = None
        for a in range(3):
            at = a * channels + tile * lanes
            part = shifted(parts[:, at : at + lanes].reshape(cols, total, lanes), a - 2)
            summed = part if summed is None else summed + part
        add_row(cells, sum_ref, tile, row, summed, total)


def outer_ahead(cells, cells_ref, place, row, kernel_ref, sum_ref, total):
    cols, channels = cells.cols, kernel_ref.shape[4]
    wide = sum_ref.shape[0] * lanes
    b = 2 * place
    weights = stacked_weights(
        kernel_ref, wide, [[(2 - s, 2 - b, 2 - c) for s in range(3) for c in range(3)]]
    )
    left = end_row(cells, cells_ref, place, 0, channels // lanes, 0, cols + 2, total)
    parts = lax.dot_general(left, weights, (((1,), (1,)), ((), ())), preferred_element_type=f32)
    for tile in range(wide // lanes):
        summed = None
        for s in range(3):
            part = None
            for c in range(3):
                at = (s * 3 + c) * wide + tile * lanes
                piece = parts[c * total : (c + cols) * total, at : at + lanes]
                part = piece if part is None else part + piece
            part = shifted(part.reshape(cols, total, lanes), s)
            summed = part if summed is None else summed + part
        add_row(cells, sum_ref, tile, row, summed, total)


def gathered(peers, frame, block_refs, start, width, channels):
    me = lax.axis_index("tm")
    wide = block_refs[0].shape[2] - start
    summed = None
    for step in range(peers):
        spread = spread_matrix(got_from(me, step, peers), width, channels, wide)
        part = jnp.dot(
            block_refs[step][frame, :, start:], spread, preferred_element_type=f32
        )
        summed = part if summed is None else summed + part
    return summed


def join_cells(flat_ref, in_ref, frame):
    rows = in_ref.shape[2]
    for col in range(in_ref.shape[1]):
        flat_ref[col * rows : (col + 1) * rows, :] = in_ref[frame, col].astype(f32)
    return flat_ref[...]


def split_cells(flat_ref, values, out_ref, frame):
    flat_ref[...] = values
    rows = out_ref.shape[2]
    for col in range(out_ref.shape[1]):
        out_ref[frame, col] = flat_ref[col * rows : (col + 1) * rows, :].astype(bf16)


def middle_kernel(peers, width, *refs):
    blocks = refs[:peers]
    gain_ref, bias_ref, out_ref = refs[peers:]
    frames, _, channels = out_ref.shape
    for frame in range(frames):
        hidden = blocks[0][frame, :, :channels].astype(f32)
        for step in range(1, peers):
            hidden = hidden + blocks[step][frame, :, :channels].astype(f32)
        hidden = hidden + bias_ref[...]
        back = gathered(peers, frame, blocks, channels, width, channels)
        inv, normed, act = rms_parts(hidden, gain_ref[...])
        out_ref[frame] = rms_back(back * silu_slope(act), inv, normed, gain_ref[...]).astype(bf16)


def final_kernel(peers, width, *refs):
    blocks = refs[:peers]
    feat_ref, reward_ref, gain_ref, out_ref, flat_ref = refs[peers:]
    frames, channels = out_ref.shape[0], out_ref.shape[3]
    for frame in range(frames):
        back = gathered(peers, frame, blocks, 0, width, channels)
        values = join_cells(flat_ref.at[frame, 0], feat_ref, frame)
        reward = join_cells(flat_ref.at[frame, 1], reward_ref, frame)
        inv, normed, act = rms_parts(values, gain_ref[...])
        result = rms_back(back * silu_slope(act), inv, normed, gain_ref[...])
        split_cells(flat_ref.at[frame, 2], result + reward, out_ref, frame)


def size_of(structs):
    return sum(math.prod(s.shape) * s.dtype.itemsize for s in structs)


def call(kernel, outs, scratch=(), flops=0, spare=2, covered=0):
    def run(*operands):
        held = size_of(outs) + size_of(operands)
        grant = 2 * held + size_of(scratch) + spare * 2**20
        return pl.pallas_call(
            kernel,
            out_shape=outs,
            scratch_shapes=list(scratch),
            cost_estimate=pl.CostEstimate(
                flops=flops + covered, bytes_accessed=held, transcendentals=0
            ),
            compiler_params=pltpu.CompilerParams(vmem_limit_bytes=min(grant, 60 * 2**20)),
        )(*operands)

    return run


def steps(
    features, reward_grad, first_kernel, second_kernel, first_gain, second_gain, first_bias
):
    peers = lax.axis_size("tm")
    frames, rows, cols, channels = features.shape
    width = first_kernel.shape[3]
    wide = -(-width // lanes) * lanes
    total = peers * frames
    plane = (rows + 2) * (cols + 2)
    count = rows * cols
    struct = jax.ShapeDtypeStruct

    cells = Cells(rows, cols)
    by_col = (0, 2, 1, 3)
    held = features.transpose(by_col), reward_grad.transpose(by_col)
    ahead_scratch = [
        pltpu.VMEM((rows + 2, (cols + 2) * total, channels), bf16),
        pltpu.VMEM((9 * wide // lanes, chunk_rows(rows, total) * (cols + 2) * total, lanes), f32),
    ]
    flops = 2 * 27 * width * channels * total * count
    sum_shapes = [
        (channels // lanes, count * total, lanes),
        (wide // lanes, count * total, lanes),
    ]

    def convolved(blocks, kernels):
        behind = len(kernels) == 2
        shapes = sum_shapes[-len(kernels) :]
        tiles = blocks[0].shape[2] // lanes
        sides, ends = halo_edges(blocks, rows)
        taps = [pltpu.VMEM((rows + 2, cols * total, 3 * wide), bf16)] if behind else []
        sums = call(
            functools.partial(inner_kernel, peers, frames, cells, len(sides), behind),
            [struct(shape, f32) for shape in shapes],
            [pltpu.VMEM((tiles, plane * total, lanes), f32), *ahead_scratch, *taps],
            flops * len(kernels),
            spare=8,
        )(*blocks, *sides, *kernels)
        return call(
            functools.partial(outer_kernel, peers, frames, cells, len(ends), behind),
            [struct((frames, count, sum(s[0] for s in shapes) * lanes), bf16)] * peers,
            [
                pltpu.VMEM((tiles, 2 * (cols + 2) * total, lanes), f32),
                *[pltpu.VMEM(shape, f32) for shape in shapes],
            ],
            flops * len(kernels) // 6,
            spare=8,
        )(*ends, *kernels, *sums)

    packed = call(
        functools.partial(pack_kernel, peers, width),
        [struct((frames, count, channels + wide), bf16)] * peers,
        [pltpu.VMEM((frames, 2, count, channels), f32)],
        covered=4 * 10**9,
    )(jnp.stack(held), first_gain)
    sums = convolved(tm_exchange(packed), [first_kernel, second_kernel])
    got = tm_exchange(sums)
    hidden_grad = call(
        functools.partial(middle_kernel, peers, width), [struct((frames, count, channels), bf16)]
    )(*got, second_gain, first_bias)[0]
    backs = convolved(tm_exchange([hidden_grad] * peers), [first_kernel])
    got = tm_exchange(backs)
    result = call(
        functools.partial(final_kernel, peers, width),
        [struct(held[0].shape, bf16)],
        [pltpu.VMEM((frames, 3, count, channels), f32)],
    )(*got, *held, first_gain)[0]
    return result.transpose(by_col)


def solution(mesh):
    in_specs = (
        P("tm", "row", "col", None),
        P("tm", "row", "col", None),
        P(None, None, None, "tm", None),
        P(None, None, None, "tm", None),
        P(),
        P(),
        P(),
    )
    out_specs = P("tm", "row", "col", None)
    return jax.shard_map(steps, mesh=mesh, in_specs=in_specs, out_specs=out_specs, check_vma=False)
```
